1024 devices in a mesh: expert: 64 (over x, z_lo, core), tensor: 16 (over z_hi, y).
Axes of the slice: x: 4, y: 4, z: 32 (z_hi: 4, z_lo: 8; z = z_hi * 8 + z_lo), core: 2. Of those that a mesh axis runs over, the one named last changes fastest.
Arguments:
- tokens: bfloat16 [8192, 2560], P(('expert', 'tensor')), may hold values from -12 to 12
- expert_ids: int32 [8192], P(('expert', 'tensor')), may hold values from 0 to 63, as said below
- slot_ids: int32 [8192], P(('expert', 'tensor')), may hold values from 0 to 3
- router: bfloat16 [2560, 64], replicated, may hold values from -0.125 to 0.125
- w_gate: bfloat16 [64, 2560, 4096], P('expert', None, 'tensor'), may hold values from -0.125 to 0.125
- w_up: bfloat16 [64, 2560, 4096], P('expert', None, 'tensor'), may hold values from -0.125 to 0.125
- hidden_grad: bfloat16 [64, 256, 4096], P('expert', None, 'tensor'), may hold values from -6 to 6
Outputs:
- activation: bfloat16 [64, 256, 4096], P('expert', None, 'tensor')
- token_grad: bfloat16 [8192, 2560], P(('expert', 'tensor'))
The draws below stay inside these ranges and needn't reach their ends.
Inputs may be any that keep to these rules, and one draw needn't show every extreme that they name: expert_ids and slot_ids are drawn together. Within each aligned group of 128 consecutive tokens no two tokens share both expert and slot, so a group sends at most 4 tokens to one expert; in every draw one expert takes all 4 slots of every group.
All inputs are finite; a program needn't handle non-finite values.
Results may differ from the reference program's by a relative error of at most 0.02.
Values may be sent and summed in bfloat16 or wider, within the bound.
No kernel may reach another device: no remote copies, remote signals or barrier semaphores. Data moves between devices by JAX's collectives and lax.ppermute only.
A program may use at most 32 MiB of HBM per device.

```python
import jax
import jax.numpy as jnp
from jax import lax

D = 2560
HID = 4096
EXPERTS = 64
TOKENS = 8192
GROUP = 128
CAP = 4
ROWS = 256
N_TENSOR = 16


def routing_pair(key):
    base_key = jax.random.fold_in(key, 17)
    full_expert = jax.random.randint(jax.random.fold_in(base_key, 1), (), 0, EXPERTS)

    def one_group(group_key):
        rank_table = jax.random.permutation(group_key, EXPERTS * CAP).astype(jnp.int32)
        slot_grid = jnp.arange(EXPERTS * CAP, dtype=jnp.int32)
        extra_expert = jax.random.randint(jax.random.fold_in(group_key, 3), (), 0, EXPERTS)
        favoured = (slot_grid // CAP == full_expert) | (slot_grid // CAP == extra_expert)
        priority = jnp.where(favoured, rank_table - EXPERTS * CAP, rank_table)
        ordering = jnp.argsort(priority, stable=True)
        chosen_ids = ordering[:GROUP]
        shuffle = jax.random.permutation(jax.random.fold_in(group_key, 5), GROUP)
        chosen_ids = chosen_ids[shuffle].astype(jnp.int32)
        return (chosen_ids // CAP, chosen_ids % CAP)
    group_keys = jax.random.split(jax.random.fold_in(base_key, 2), TOKENS // GROUP)
    expert_table, slot_table = jax.vmap(one_group)(group_keys)
    return (expert_table.reshape(TOKENS).astype(jnp.int32), slot_table.reshape(TOKENS).astype(jnp.int32))


def draw_expert_ids(key, part):
    return routing_pair(key)[0]


def draw_slot_ids(key, part):
    return routing_pair(key)[1]


def levels(own_key, shape, cuts, low, high):
    gain, own = 1.0, jax.random.fold_in(own_key, 6)
    for dim, blocks in cuts:
        heights = jnp.exp(jax.random.uniform(jax.random.fold_in(own, dim), (blocks,), jnp.float32, low / len(cuts), high / len(cuts)))
        gain = gain * jnp.repeat(heights, shape[dim] // blocks).reshape([-1 if axis == dim else 1 for axis in range(len(shape))])
    return gain


def gaussian(own_key, extent, deviation, most, cuts=(), kind=jnp.bfloat16):
    entries = deviation * jax.random.normal(own_key, extent, jnp.float32)
    if cuts:
        entries = entries * levels(own_key, extent, cuts, -0.22, 0.18)
    return jnp.clip(entries, -most, most).astype(kind)


def setup_inputs(seed: int = 0) -> dict:
    keys = jax.random.split(jax.random.key(seed), 8)
    return {
        "tokens": gaussian(keys[0], (TOKENS, D), 2.0, 12.0, ((0, 1024),)),
        "expert_ids": draw_expert_ids(jax.random.fold_in(keys[7], 71), 0),
        "slot_ids": draw_slot_ids(jax.random.fold_in(keys[7], 71), 0),
        "router": gaussian(keys[3], (D, EXPERTS), D ** -0.5, 0.125),
        "w_gate": gaussian(keys[4], (EXPERTS, D, HID), D ** -0.5, 0.125, ((0, 64), (2, 16))),
        "w_up": gaussian(keys[5], (EXPERTS, D, HID), D ** -0.5, 0.125, ((0, 64), (2, 16))),
        "hidden_grad": gaussian(keys[6], (EXPERTS, ROWS, HID), 1.0, 6.0, ((0, 64), (2, 16))),
    }


def silu_parts(gate_proj):
    sigma_gate = jax.nn.sigmoid(gate_proj)
    return gate_proj * sigma_gate, sigma_gate * (1.0 + gate_proj * (1.0 - sigma_gate))


def reference(tokens, expert_ids, slot_ids, router, w_gate, w_up, hidden_grad):
    logits = jnp.dot(tokens, router, preferred_element_type=jnp.float32)
    picked = jnp.take_along_axis(logits, expert_ids[:, None], axis=1)[:, 0]
    router_score = jax.nn.sigmoid(picked)
    routed_in = (router_score[:, None] * tokens.astype(jnp.float32)).astype(jnp.bfloat16)
    group_index = (jnp.arange(TOKENS, dtype=jnp.int32) // GROUP).astype(jnp.int32)
    target_row = (expert_ids * ROWS + group_index * CAP + slot_ids).astype(jnp.int32)
    dispatched = jnp.zeros((EXPERTS * ROWS, D), jnp.bfloat16).at[target_row].set(routed_in)
    dispatched = dispatched.reshape(EXPERTS, ROWS, D)
    hidden_piece = HID // N_TENSOR

    def per_expert(expert_item):
        routed_rows, gate_weight, up_weight, cotangent = expert_item
        gate_proj = jnp.dot(routed_rows, gate_weight, preferred_element_type=jnp.float32)
        lifted = jnp.dot(routed_rows, up_weight, preferred_element_type=jnp.float32)
        silu_gate, silu_slope = silu_parts(gate_proj)
        activation = (silu_gate * lifted).astype(jnp.bfloat16)
        cot_float = cotangent.astype(jnp.float32)
        d_gate = (cot_float * lifted * silu_slope).astype(jnp.bfloat16)
        d_lifted = (cot_float * silu_gate).astype(jnp.bfloat16)
        gate_blocks = d_gate.astype(jnp.float32).reshape(ROWS, N_TENSOR, hidden_piece)
        lift_blocks = d_lifted.astype(jnp.float32).reshape(ROWS, N_TENSOR, hidden_piece)
        gate_table = gate_weight.astype(jnp.float32).reshape(D, N_TENSOR, hidden_piece)
        up_table = up_weight.astype(jnp.float32).reshape(D, N_TENSOR, hidden_piece)
        partial_value = jnp.einsum('rtk,dtk->trd', gate_blocks, gate_table) + jnp.einsum('rtk,dtk->trd', lift_blocks, up_table)
        partial_value = lax.optimization_barrier(partial_value.astype(jnp.bfloat16)).astype(jnp.float32)
        d_rows = jnp.sum(partial_value, axis=0).astype(jnp.bfloat16)
        return activation, d_rows

    activation, d_dispatched = lax.map(per_expert, (dispatched, w_gate, w_up, hidden_grad))
    d_routed = d_dispatched.reshape(EXPERTS * ROWS, D)[target_row]
    d_float = d_routed.astype(jnp.float32)
    inner = jnp.sum(tokens.astype(jnp.float32) * d_float, axis=1)
    router_column = router.astype(jnp.float32).T[expert_ids]
    gradient = router_score[:, None] * d_float + (inner * router_score * (1.0 - router_score))[:, None] * router_column
    return activation, gradient.astype(jnp.bfloat16)
```

```python
import math

import jax
import jax.numpy as jnp
from jax import lax
from jax.sharding import Mesh
from jax.sharding import PartitionSpec as P

CODE_COLUMNS = 128


def exchange(buffer, axes):
    return lax.all_to_all(buffer, axes, split_axis=0, concat_axis=0, tiled=True)


def shards(tokens, expert_ids, slot_ids, router, w_gate, w_up, hidden_grad):
    n_high, n_row, n_expert = lax.axis_size("high"), lax.axis_size("row"), lax.axis_size("expert")
    n_tensor = n_high * n_row
    tok_rows, width = tokens.shape
    experts_all = router.shape[1]
    rows_all = hidden_grad.shape[1]
    capacity = rows_all // n_expert
    piece = width // n_row
    group = n_tensor * tok_rows
    gate_weight, up_weight = w_gate[0], w_up[0]

    logits = jnp.dot(tokens, router, preferred_element_type=jnp.float32)
    picked_mask = expert_ids[:, None] == jnp.arange(experts_all, dtype=jnp.int32)[None, :]
    picked = jnp.sum(jnp.where(picked_mask, logits, 0.0), axis=1)
    router_score = jax.nn.sigmoid(picked)
    token_float = tokens.astype(jnp.float32)
    routed_in = (router_score[:, None] * token_float).astype(jnp.bfloat16)

    code = (expert_ids * capacity + slot_ids).astype(jnp.bfloat16)
    pieces = routed_in.reshape(tok_rows, n_row, piece).transpose(1, 0, 2)
    codes = jnp.broadcast_to(code[None, :, None], (n_row, tok_rows, CODE_COLUMNS))
    outgoing = jnp.concatenate([pieces, codes], axis=2)
    outgoing = jnp.broadcast_to(outgoing[None], (n_high,) + outgoing.shape)
    outgoing = outgoing.reshape(n_tensor, tok_rows, piece + CODE_COLUMNS)
    group_rows = exchange(outgoing, ("high", "row")).reshape(group, piece + CODE_COLUMNS)

    slot_numbers = jnp.arange(experts_all * capacity, dtype=jnp.int32)
    placed = group_rows[:, piece : piece + 1].astype(jnp.int32) == slot_numbers[None, :]
    placed = placed.astype(jnp.bfloat16)
    slots = lax.dot_general(
        placed, group_rows[:, :piece], (((0,), (0,)), ((), ())), preferred_element_type=jnp.float32
    ).astype(jnp.bfloat16)
    arrived = exchange(slots.reshape(experts_all, capacity, piece), "expert").reshape(rows_all, piece)
    arrived = exchange(jnp.broadcast_to(arrived[None], (n_row, rows_all, piece)), "row")

    gate_proj = jnp.zeros((rows_all, gate_weight.shape[1]), jnp.float32)
    lifted = gate_proj
    for y in range(n_row):
        cut = slice(y * piece, (y + 1) * piece)
        gate_proj += jnp.dot(arrived[y], gate_weight[cut], preferred_element_type=jnp.float32)
        lifted += jnp.dot(arrived[y], up_weight[cut], preferred_element_type=jnp.float32)
    sigma_gate = jax.nn.sigmoid(gate_proj)
    silu_gate = gate_proj * sigma_gate
    silu_slope = sigma_gate * (1.0 + gate_proj * (1.0 - sigma_gate))
    activation = (silu_gate * lifted).astype(jnp.bfloat16)
    cotangent = hidden_grad[0].astype(jnp.float32)
    d_gate = (cotangent * lifted * silu_slope).astype(jnp.bfloat16)
    d_lifted = (cotangent * silu_gate).astype(jnp.bfloat16)
    contract = (((1,), (1,)), ((), ()))
    partial = []
    for y in range(n_row):
        cut = slice(y * piece, (y + 1) * piece)
        part = lax.dot_general(d_gate, gate_weight[cut], contract, preferred_element_type=jnp.float32)
        part += lax.dot_general(d_lifted, up_weight[cut], contract, preferred_element_type=jnp.float32)
        partial.append(part.astype(jnp.bfloat16))

    partial = exchange(jnp.stack(partial), "row")
    summed = jnp.sum(partial.astype(jnp.float32), axis=0).astype(jnp.bfloat16)
    returned = exchange(summed.reshape(n_expert, capacity, piece), "expert").reshape(experts_all * capacity, piece)
    mine = jnp.dot(placed, returned, preferred_element_type=jnp.float32).astype(jnp.bfloat16)
    home = exchange(mine.reshape(n_tensor, tok_rows, piece), ("high", "row"))
    home = jnp.sum(home.reshape(n_high, n_row, tok_rows, piece).astype(jnp.float32), axis=0)
    d_float = home.transpose(1, 0, 2).reshape(tok_rows, width).astype(jnp.bfloat16).astype(jnp.float32)

    inner = jnp.sum(token_float * d_float, axis=1)
    router_column = lax.dot_general(
        picked_mask.astype(jnp.bfloat16), router, contract, preferred_element_type=jnp.float32
    )
    gradient = (
        router_score[:, None] * d_float
        + (inner * router_score * (1.0 - router_score))[:, None] * router_column
    )
    return activation[None], gradient.astype(jnp.bfloat16)


def solution(mesh):
    n_expert, n_tensor = mesh.devices.shape
    n_row = math.isqrt(n_tensor)
    split = Mesh(mesh.devices.reshape(n_expert, n_tensor // n_row, n_row), ("expert", "high", "row"))
    tensor = ("high", "row")
    owners = ("expert", "high", "row")
    in_specs = (
        P(owners, None),
        P(owners),
        P(owners),
        P(),
        P("expert", None, tensor),
        P("expert", None, tensor),
        P("expert", None, tensor),
    )
    out_specs = (P("expert", None, tensor), P(owners, None))
    return jax.shard_map(shards, mesh=split, in_specs=in_specs, out_specs=out_specs, check_vma=False)
```

```python
import math

import jax
import jax.numpy as jnp
from jax import lax
from jax.sharding import Mesh
from jax.sharding import PartitionSpec as P

CODE_COLUMNS = 128


def exchange(buffer, axes):
    return lax.all_to_all(buffer, axes, split_axis=0, concat_axis=0, tiled=True)


def swap_rows(rows, outer, inner, unit):
    out = lax.broadcasted_iota(jnp.int32, (rows, rows), 0)
    source = (out // unit % inner * outer + out // (unit * inner)) * unit + out % unit
    return (source == lax.broadcasted_iota(jnp.int32, (rows, rows), 1)).astype(jnp.bfloat16)


def shards(tokens, expert_ids, slot_ids, router, w_gate, w_up, hidden_grad):
    n_high, n_row = lax.axis_size("high"), lax.axis_size("row")
    n_x, n_pair = lax.axis_size("x"), lax.axis_size("pair")
    n_tensor, n_expert = n_high * n_row, n_x * n_pair
    tok_rows, width = tokens.shape
    experts_all = router.shape[1]
    rows_all = hidden_grad.shape[1]
    capacity = rows_all // n_expert
    piece = width // n_row
    group = n_tensor * tok_rows
    gate_weight, up_weight = w_gate[0], w_up[0]

    logits = jnp.dot(tokens, router, preferred_element_type=jnp.float32)
    picked_mask = expert_ids[:, None] == jnp.arange(experts_all, dtype=jnp.int32)[None, :]
    picked = jnp.sum(jnp.where(picked_mask, logits, 0.0), axis=1)
    router_score = jax.nn.sigmoid(picked)
    token_float = tokens.astype(jnp.float32)
    routed_in = (router_score[:, None] * token_float).astype(jnp.bfloat16)

    code = ((expert_ids % n_pair * n_x + expert_ids // n_pair) * capacity + slot_ids).astype(jnp.bfloat16)
    pieces = routed_in.reshape(tok_rows, n_row, piece).transpose(1, 0, 2)
    codes = jnp.broadcast_to(code[None, :, None], (n_row, tok_rows, CODE_COLUMNS))
    outgoing = jnp.concatenate([pieces, codes], axis=2)
    outgoing = jnp.broadcast_to(outgoing[None], (n_high,) + outgoing.shape)
    outgoing = outgoing.reshape(n_tensor, tok_rows, piece + CODE_COLUMNS)
    group_rows = exchange(outgoing, ("high", "row")).reshape(group, piece + CODE_COLUMNS)

    slot_numbers = jnp.arange(experts_all * capacity, dtype=jnp.int32)
    placed = group_rows[:, piece : piece + 1].astype(jnp.int32) == slot_numbers[None, :]
    placed = placed.astype(jnp.bfloat16)
    slots = lax.dot_general(
        placed, group_rows[:, :piece], (((0,), (0,)), ((), ())), preferred_element_type=jnp.float32
    ).astype(jnp.bfloat16)
    planes = exchange(slots.reshape(n_pair, n_x * capacity, piece), "pair").reshape(rows_all, piece)
    x_first = swap_rows(rows_all, n_x, n_pair, capacity)
    planes = jnp.dot(x_first, planes, preferred_element_type=jnp.float32).astype(jnp.bfloat16)
    block = n_pair * capacity
    planes = jnp.broadcast_to(planes.reshape(1, n_x, block, piece), (n_row, n_x, block, piece))
    arrived = exchange(planes.reshape(n_row * n_x, block, piece), ("row", "x"))
    arrived = arrived.reshape(n_row, rows_all, piece)

    gate_proj = jnp.zeros((rows_all, gate_weight.shape[1]), jnp.float32)
    lifted = gate_proj
    for y in range(n_row):
        cut = slice(y * piece, (y + 1) * piece)
        gate_proj += jnp.dot(arrived[y], gate_weight[cut], preferred_element_type=jnp.float32)
        lifted += jnp.dot(arrived[y], up_weight[cut], preferred_element_type=jnp.float32)
    sigma_gate = jax.nn.sigmoid(gate_proj)
    silu_gate = gate_proj * sigma_gate
    silu_slope = sigma_gate * (1.0 + gate_proj * (1.0 - sigma_gate))
    activation = (silu_gate * lifted).astype(jnp.bfloat16)
    cotangent = hidden_grad[0].astype(jnp.float32)
    d_gate = (cotangent * lifted * silu_slope).astype(jnp.bfloat16)
    d_lifted = (cotangent * silu_gate).astype(jnp.bfloat16)
    contract = (((1,), (1,)), ((), ()))
    partial = []
    for y in range(n_row):
        cut = slice(y * piece, (y + 1) * piece)
        part = lax.dot_general(d_gate, gate_weight[cut], contract, preferred_element_type=jnp.float32)
        part += lax.dot_general(d_lifted, up_weight[cut], contract, preferred_element_type=jnp.float32)
        partial.append(part.astype(jnp.bfloat16))

    partial = exchange(jnp.stack(partial).reshape(n_row * n_x, block, piece), ("row", "x"))
    summed = jnp.sum(partial.reshape(n_row, rows_all, piece).astype(jnp.float32), axis=0).astype(jnp.bfloat16)
    pair_first = swap_rows(rows_all, n_pair, n_x, capacity)
    summed = jnp.dot(pair_first, summed, preferred_element_type=jnp.float32).astype(jnp.bfloat16)
    returned = exchange(summed.reshape(n_pair, n_x * capacity, piece), "pair").reshape(experts_all * capacity, piece)
    mine = jnp.dot(placed, returned, preferred_element_type=jnp.float32).astype(jnp.bfloat16)
    home = exchange(mine.reshape(n_tensor, tok_rows, piece), ("high", "row"))
    home = jnp.sum(home.reshape(n_high, n_row, tok_rows, piece).astype(jnp.float32), axis=0)
    d_float = home.transpose(1, 0, 2).reshape(tok_rows, width).astype(jnp.bfloat16).astype(jnp.float32)

    inner = jnp.sum(token_float * d_float, axis=1)
    router_column = lax.dot_general(
        picked_mask.astype(jnp.bfloat16), router, contract, preferred_element_type=jnp.float32
    )
    gradient = (
        router_score[:, None] * d_float
        + (inner * router_score * (1.0 - router_score))[:, None] * router_column
    )
    return activation[None], gradient.astype(jnp.bfloat16)


def solution(mesh):
    n_expert, n_tensor = mesh.devices.shape
    n_row = n_x = math.isqrt(n_tensor)
    axes = ("x", "pair", "high", "row")
    split = Mesh(mesh.devices.reshape(n_x, n_expert // n_x, n_tensor // n_row, n_row), axes)
    expert, tensor = axes[:2], axes[2:]
    in_specs = (
        P(axes, None),
        P(axes),
        P(axes),
        P(),
        P(expert, None, tensor),
        P(expert, None, tensor),
        P(expert, None, tensor),
    )
    out_specs = (P(expert, None, tensor), P(axes, None))
    return jax.shard_map(shards, mesh=split, in_specs=in_specs, out_specs=out_specs, check_vma=False)
```

```python
import itertools
import math

import jax
import jax.numpy as jnp
from jax import lax
from jax.sharding import Mesh
from jax.sharding import PartitionSpec as P

CODE_COLUMNS = 128


AXES = ("x", "low", "core", "high", "row")


def exchange(buffer, axes, groups=None):
    return lax.all_to_all(buffer, axes, split_axis=0, concat_axis=0, axis_index_groups=groups, tiled=True)


def window_groups():
    n_x, n_low, n_core, n_high, n_row = (lax.axis_size(axis) for axis in AXES)
    groups = []
    for core, high, row in itertools.product(range(n_core), range(n_high), range(n_row)):
        group = []
        for x, low in itertools.product(range(n_x), range(n_low)):
            run = (high + (core == 1 and low < n_low // 2)) % n_high
            group.append((((x * n_low + low) * n_core + core) * n_high + run) * n_row + row)
        groups.append(group)
    return groups


def swap_rows(rows, outer, inner, unit):
    out = lax.broadcasted_iota(jnp.int32, (rows, rows), 0)
    source = (out // unit % inner * outer + out // (unit * inner)) * unit + out % unit
    return (source == lax.broadcasted_iota(jnp.int32, (rows, rows), 1)).astype(jnp.bfloat16)


def reorder(matrix, rows):
    return jnp.dot(matrix, rows, preferred_element_type=jnp.float32).astype(jnp.bfloat16)


def shards(tokens, expert_ids, slot_ids, router, w_gate, w_up, hidden_grad):
    n_x, n_low, n_core, n_high, n_row = (lax.axis_size(axis) for axis in AXES)
    n_chip, n_tensor = n_x * n_low, n_high * n_row
    n_expert = n_chip * n_core
    tok_rows, width = tokens.shape
    experts_all = router.shape[1]
    rows_all = hidden_grad.shape[1]
    capacity = rows_all // n_expert
    piece = width // n_row
    group = n_tensor * tok_rows
    gate_weight, up_weight = w_gate[0], w_up[0]

    logits = jnp.dot(tokens, router, preferred_element_type=jnp.float32)
    picked_mask = expert_ids[:, None] == jnp.arange(experts_all, dtype=jnp.int32)[None, :]
    picked = jnp.sum(jnp.where(picked_mask, logits, 0.0), axis=1)
    router_score = jax.nn.sigmoid(picked)
    token_float = tokens.astype(jnp.float32)
    routed_in = (router_score[:, None] * token_float).astype(jnp.bfloat16)

    code = (expert_ids * capacity + slot_ids).astype(jnp.bfloat16)
    pieces = routed_in.reshape(tok_rows, n_row, piece).transpose(1, 0, 2)
    codes = jnp.broadcast_to(code[None, :, None], (n_row, tok_rows, CODE_COLUMNS))
    outgoing = jnp.concatenate([pieces, codes], axis=2)
    outgoing = jnp.broadcast_to(outgoing[None], (n_high,) + outgoing.shape)
    outgoing = outgoing.reshape(n_tensor, tok_rows, piece + CODE_COLUMNS)
    group_rows = exchange(outgoing, ("high", "row")).reshape(group, piece + CODE_COLUMNS)

    slot_numbers = jnp.arange(experts_all * capacity, dtype=jnp.int32)
    placed = group_rows[:, piece : piece + 1].astype(jnp.int32) == slot_numbers[None, :]
    placed = placed.astype(jnp.bfloat16)
    slots = lax.dot_general(
        placed, group_rows[:, :piece], (((0,), (0,)), ((), ())), preferred_element_type=jnp.float32
    ).astype(jnp.bfloat16)
    groups = window_groups()
    core_first = swap_rows(rows_all, n_core, n_chip, capacity)
    chip_first = swap_rows(rows_all, n_chip, n_core, capacity)
    half = rows_all // n_core
    chips = exchange(slots.reshape(n_chip, n_core * capacity, piece), AXES, groups)
    chips = reorder(core_first, chips.reshape(rows_all, piece)).reshape(1, n_core, half, piece)
    chips = jnp.broadcast_to(chips, (n_row, n_core, half, piece)).reshape(n_row * n_core, half, piece)
    arrived = exchange(chips, ("row", "core")).reshape(n_row, rows_all, piece)

    gate_proj = jnp.zeros((rows_all, gate_weight.shape[1]), jnp.float32)
    lifted = gate_proj
    for y in range(n_row):
        cut = slice(y * piece, (y + 1) * piece)
        gate_proj += jnp.dot(arrived[y], gate_weight[cut], preferred_element_type=jnp.float32)
        lifted += jnp.dot(arrived[y], up_weight[cut], preferred_element_type=jnp.float32)
    sigma_gate = jax.nn.sigmoid(gate_proj)
    silu_gate = gate_proj * sigma_gate
    silu_slope = sigma_gate * (1.0 + gate_proj * (1.0 - sigma_gate))
    activation = reorder(chip_first, (silu_gate * lifted).astype(jnp.bfloat16))
    cotangent = reorder(core_first, hidden_grad[0]).astype(jnp.float32)
    d_gate = (cotangent * lifted * silu_slope).astype(jnp.bfloat16)
    d_lifted = (cotangent * silu_gate).astype(jnp.bfloat16)
    contract = (((1,), (1,)), ((), ()))
    partial = []
    for y in range(n_row):
        cut = slice(y * piece, (y + 1) * piece)
        part = lax.dot_general(d_gate, gate_weight[cut], contract, preferred_element_type=jnp.float32)
        part += lax.dot_general(d_lifted, up_weight[cut], contract, preferred_element_type=jnp.float32)
        partial.append(part.astype(jnp.bfloat16))

    partial = exchange(jnp.stack(partial).reshape(n_row * n_core, half, piece), ("row", "core"))
    summed = jnp.sum(partial.reshape(n_row, rows_all, piece).astype(jnp.float32), axis=0).astype(jnp.bfloat16)
    summed = reorder(chip_first, summed).reshape(n_chip, n_core * capacity, piece)
    returned = exchange(summed, AXES, groups).reshape(experts_all * capacity, piece)
    mine = jnp.dot(placed, returned, preferred_element_type=jnp.float32).astype(jnp.bfloat16)
    home = exchange(mine.reshape(n_tensor, tok_rows, piece), ("high", "row"))
    home = jnp.sum(home.reshape(n_high, n_row, tok_rows, piece).astype(jnp.float32), axis=0)
    d_float = home.transpose(1, 0, 2).reshape(tok_rows, width).astype(jnp.bfloat16).astype(jnp.float32)

    inner = jnp.sum(token_float * d_float, axis=1)
    router_column = lax.dot_general(
        picked_mask.astype(jnp.bfloat16), router, contract, preferred_element_type=jnp.float32
    )
    gradient = (
        router_score[:, None] * d_float
        + (inner * router_score * (1.0 - router_score))[:, None] * router_column
    )
    return activation[None], gradient.astype(jnp.bfloat16)


def solution(mesh):
    n_expert, n_tensor = mesh.devices.shape
    n_row = n_x = math.isqrt(n_tensor)
    split = Mesh(mesh.devices.reshape(n_x, n_expert // (2 * n_x), 2, n_tensor // n_row, n_row), AXES)
    expert, tensor = AXES[:3], AXES[3:]
    in_specs = (
        P(AXES, None),
        P(AXES),
        P(AXES),
        P(),
        P(expert, None, tensor),
        P(expert, None, tensor),
        P(expert, None, tensor),
    )
    out_specs = (P(expert, None, tensor), P(AXES, None))
    return jax.shard_map(shards, mesh=split, in_specs=in_specs, out_specs=out_specs, check_vma=False)
```

```python
import functools
import itertools
import math

import jax
import jax.numpy as jnp
from jax import lax
from jax.experimental import pallas as pl
from jax.experimental.pallas import tpu as pltpu
from jax.sharding import Mesh
from jax.sharding import PartitionSpec as P

CODE_COLUMNS = 128
WHOLE_VMEM = 66_500_000


AXES = ("x", "low", "core", "high", "row")


def exchange(buffer, axes, groups=None):
    return lax.all_to_all(buffer, axes, split_axis=0, concat_axis=0, axis_index_groups=groups, tiled=True)


def window_groups():
    n_x, n_low, n_core, n_high, n_row = (lax.axis_size(axis) for axis in AXES)
    groups = []
    for core, high, row in itertools.product(range(n_core), range(n_high), range(n_row)):
        group = []
        for x, low in itertools.product(range(n_x), range(n_low)):
            run = (high + (core == 1 and low < n_low // 2)) % n_high
            group.append((((x * n_low + low) * n_core + core) * n_high + run) * n_row + row)
        groups.append(group)
    return groups


def swap_rows(rows, outer, inner, unit):
    out = lax.broadcasted_iota(jnp.int32, (rows, rows), 0)
    source = (out // unit % inner * outer + out // (unit * inner)) * unit + out % unit
    return (source == lax.broadcasted_iota(jnp.int32, (rows, rows), 1)).astype(jnp.bfloat16)


def product(left, right, contract=(1, 0)):
    return lax.dot_general(
        left, right, (((contract[0],), (contract[1],)), ((), ())), preferred_element_type=jnp.float32
    )


def column(row):
    n = row.shape[1]
    diagonal = lax.broadcasted_iota(jnp.int32, (n, n), 0) == lax.broadcasted_iota(jnp.int32, (n, n), 1)
    values = jnp.broadcast_to(row.astype(jnp.float32), (n, n))
    return jnp.sum(jnp.where(diagonal, values, 0.0), axis=1, keepdims=True)


def send_kernel(n_row, capacity, *refs):
    sources, (out_ref, score_ref), buffers, sems = refs[:4], refs[4:6], refs[6:10], refs[10]
    copies = [pltpu.make_async_copy(sources[i], buffers[i], sems.at[i]) for i in range(4)]
    for copy in copies:
        copy.start()
    for copy in copies:
        copy.wait()
    tokens_ref, expert_ref, slot_ref, router_ref = buffers
    tok_rows, width = tokens_ref.shape
    piece = width // n_row
    experts = column(expert_ref[...])
    code = experts * capacity + column(slot_ref[...])
    logits = product(tokens_ref[...], router_ref[...], (1, 1))
    numbers = lax.broadcasted_iota(jnp.int32, logits.shape, 1).astype(jnp.float32)
    picked = jnp.sum(jnp.where(numbers == experts, logits, 0.0), axis=1, keepdims=True)
    score = jax.nn.sigmoid(picked)
    score_ref[...] = jnp.broadcast_to(score, score_ref.shape)
    codes = jnp.broadcast_to(code, (tok_rows, CODE_COLUMNS)).astype(jnp.bfloat16)
    for y in range(n_row):
        cut = pl.ds(y * piece, piece)
        scaled = (score * tokens_ref[:, cut].astype(jnp.float32)).astype(jnp.bfloat16)
        for high in range(out_ref.shape[0] // n_row):
            out_ref[high * n_row + y, :, pl.ds(0, piece)] = scaled
            out_ref[high * n_row + y, :, pl.ds(piece, CODE_COLUMNS)] = codes


def spread_kernel(order, rows_ref, out_ref):
    ordered = product(swap_rows(*order), rows_ref[...]).astype(jnp.bfloat16)
    for y in range(out_ref.shape[0]):
        out_ref[y] = ordered


def collect_kernel(order, parts_ref, out_ref):
    swap = swap_rows(*order)
    total = product(swap, parts_ref[0])
    for y in range(1, parts_ref.shape[0]):
        total += product(swap, parts_ref[y])
    out_ref[...] = total.astype(jnp.bfloat16)


def expert_kernel(order, back, rows_ref, hidden_ref, gate_ref, up_ref, act_ref, out_ref):
    n_row, _, piece = rows_ref.shape
    cuts = [pl.ds(y * piece, piece) for y in range(n_row)]
    cotangent = product(swap_rows(*order), hidden_ref[...])
    gate_proj = jnp.zeros(act_ref.shape, jnp.float32)
    lifted = gate_proj
    for y in range(n_row):
        gate_proj += product(rows_ref[y], gate_ref[cuts[y], :])
        lifted += product(rows_ref[y], up_ref[cuts[y], :])
    sigma_gate = jax.nn.sigmoid(gate_proj)
    silu_gate = gate_proj * sigma_gate
    silu_slope = sigma_gate * (1.0 + gate_proj * (1.0 - sigma_gate))
    activation = (silu_gate * lifted).astype(jnp.bfloat16)
    d_gate = (cotangent * lifted * silu_slope).astype(jnp.bfloat16)
    d_lifted = (cotangent * silu_gate).astype(jnp.bfloat16)
    for y in range(n_row):
        part = product(d_gate, gate_ref[cuts[y], :], (1, 1))
        part += product(d_lifted, up_ref[cuts[y], :], (1, 1))
        out_ref[y] = part.astype(jnp.bfloat16)
    act_ref[...] = product(swap_rows(*back), activation).astype(jnp.bfloat16)


VMEM_SPEC = pl.BlockSpec(memory_space=pltpu.VMEM)


def local_call(kernel, shape, inputs, flops, limit):
    moved = 2 * (math.prod(shape) + sum(value.size for value in inputs))
    return pl.pallas_call(
        kernel,
        out_shape=jax.ShapeDtypeStruct(shape, jnp.bfloat16),
        in_specs=[VMEM_SPEC] * len(inputs),
        out_specs=VMEM_SPEC,
        compiler_params=pltpu.CompilerParams(vmem_limit_bytes=limit),
        cost_estimate=pl.CostEstimate(flops=flops, bytes_accessed=moved, transcendentals=0),
    )(*inputs)


def run_expert(order, back, rows, hidden, gate_weight, up_weight):
    n_row, rows_all, piece = rows.shape
    width, units = gate_weight.shape
    return pl.pallas_call(
        functools.partial(expert_kernel, order, back),
        out_shape=(
            jax.ShapeDtypeStruct(hidden.shape, jnp.bfloat16),
            jax.ShapeDtypeStruct(rows.shape, jnp.bfloat16),
        ),
        in_specs=[VMEM_SPEC] * 4,
        out_specs=(VMEM_SPEC, VMEM_SPEC),
        compiler_params=pltpu.CompilerParams(vmem_limit_bytes=24 << 20),
        cost_estimate=pl.CostEstimate(
            flops=8 * rows_all * width * units, bytes_accessed=4 * width * units, transcendentals=rows_all * units
        ),
    )(rows, hidden, gate_weight, up_weight)


def shards(tokens, expert_ids, slot_ids, router, w_gate, w_up, hidden_grad):
    n_x, n_low, n_core, n_high, n_row = (lax.axis_size(axis) for axis in AXES)
    n_chip, n_tensor = n_x * n_low, n_high * n_row
    n_expert = n_chip * n_core
    tok_rows, width = tokens.shape
    experts_all = router.shape[1]
    rows_all = hidden_grad.shape[1]
    capacity = rows_all // n_expert
    piece = width // n_row
    group = n_tensor * tok_rows
    gate_weight, up_weight = w_gate[0], w_up[0]

    outgoing, scores = pl.pallas_call(
        functools.partial(send_kernel, n_row, capacity),
        out_shape=(
            jax.ShapeDtypeStruct((n_tensor, tok_rows, piece + CODE_COLUMNS), jnp.bfloat16),
            jax.ShapeDtypeStruct((tok_rows, CODE_COLUMNS), jnp.float32),
        ),
        in_specs=[pl.BlockSpec(memory_space=pltpu.HBM)] * 4,
        out_specs=(VMEM_SPEC, VMEM_SPEC),
        scratch_shapes=[
            pltpu.VMEM((tok_rows, width), jnp.bfloat16),
            pltpu.VMEM((1, tok_rows), jnp.int32),
            pltpu.VMEM((1, tok_rows), jnp.int32),
            pltpu.VMEM((experts_all, width), jnp.bfloat16),
            pltpu.SemaphoreType.DMA((4,)),
        ],
        compiler_params=pltpu.CompilerParams(vmem_limit_bytes=WHOLE_VMEM),
        cost_estimate=pl.CostEstimate(
            flops=2 * tok_rows * width * experts_all, bytes_accessed=2 * width * experts_all, transcendentals=tok_rows
        ),
    )(tokens, expert_ids.reshape(1, tok_rows), slot_ids.reshape(1, tok_rows), router.T)
    router_score = scores[:, 0]
    picked_mask = expert_ids[:, None] == jnp.arange(experts_all, dtype=jnp.int32)[None, :]
    token_float = tokens.astype(jnp.float32)
    group_rows = exchange(outgoing, ("high", "row")).reshape(group, piece + CODE_COLUMNS)

    slot_numbers = jnp.arange(experts_all * capacity, dtype=jnp.int32)
    placed = group_rows[:, piece : piece + 1].astype(jnp.int32) == slot_numbers[None, :]
    placed = placed.astype(jnp.bfloat16)
    slots = lax.dot_general(
        placed, group_rows[:, :piece], (((0,), (0,)), ((), ())), preferred_element_type=jnp.float32
    ).astype(jnp.bfloat16)
    groups = window_groups()
    core_first = (rows_all, n_core, n_chip, capacity)
    chip_first = (rows_all, n_chip, n_core, capacity)
    half = rows_all // n_core
    swap_flops = 2 * rows_all * rows_all * piece
    chips = exchange(slots.reshape(n_chip, n_core * capacity, piece), AXES, groups).reshape(rows_all, piece)
    chips = local_call(
        functools.partial(spread_kernel, core_first), (n_row, rows_all, piece), [chips], swap_flops, 8 << 20
    )
    arrived = exchange(chips.reshape(n_row * n_core, half, piece), ("row", "core"))

    activation, partial = run_expert(
        core_first, chip_first, arrived.reshape(n_row, rows_all, piece), hidden_grad[0], gate_weight, up_weight
    )

    partial = exchange(partial.reshape(n_row * n_core, half, piece), ("row", "core"))
    summed = local_call(
        functools.partial(collect_kernel, chip_first),
        (rows_all, piece),
        [partial.reshape(n_row, rows_all, piece)],
        n_row * swap_flops,
        8 << 20,
    )
    summed = summed.reshape(n_chip, n_core * capacity, piece)
    returned = exchange(summed, AXES, groups).reshape(experts_all * capacity, piece)
    mine = jnp.dot(placed, returned, preferred_element_type=jnp.float32).astype(jnp.bfloat16)
    home = exchange(mine.reshape(n_tensor, tok_rows, piece), ("high", "row"))
    home = jnp.sum(home.reshape(n_high, n_row, tok_rows, piece).astype(jnp.float32), axis=0)
    d_float = home.transpose(1, 0, 2).reshape(tok_rows, width).astype(jnp.bfloat16).astype(jnp.float32)

    inner = jnp.sum(token_float * d_float, axis=1)
    router_column = lax.dot_general(
        picked_mask.astype(jnp.bfloat16), router, (((1,), (1,)), ((), ())), preferred_element_type=jnp.float32
    )
    gradient = (
        router_score[:, None] * d_float
        + (inner * router_score * (1.0 - router_score))[:, None] * router_column
    )
    return activation[None], gradient.astype(jnp.bfloat16)


def solution(mesh):
    n_expert, n_tensor = mesh.devices.shape
    n_row = n_x = math.isqrt(n_tensor)
    split = Mesh(mesh.devices.reshape(n_x, n_expert // (2 * n_x), 2, n_tensor // n_row, n_row), AXES)
    expert, tensor = AXES[:3], AXES[3:]
    in_specs = (
        P(AXES, None),
        P(AXES),
        P(AXES),
        P(),
        P(expert, None, tensor),
        P(expert, None, tensor),
        P(expert, None, tensor),
    )
    out_specs = (P(expert, None, tensor), P(AXES, None))
    return jax.shard_map(shards, mesh=split, in_specs=in_specs, out_specs=out_specs, check_vma=False)
```

```python
import functools
import itertools
import math

import jax
import jax.numpy as jnp
from jax import lax
from jax.experimental import pallas as pl
from jax.experimental.pallas import tpu as pltpu
from jax.sharding import Mesh
from jax.sharding import PartitionSpec as P

CODE_COLUMNS = 128
WHOLE_VMEM = 66_500_000


AXES = ("x", "low", "core", "high", "row")


def exchange(buffer, axes, groups=None):
    return lax.all_to_all(buffer, axes, split_axis=0, concat_axis=0, axis_index_groups=groups, tiled=True)


def window_groups():
    n_x, n_low, n_core, n_high, n_row = (lax.axis_size(axis) for axis in AXES)
    groups = []
    for x, core, high, row in itertools.product(range(n_x), range(n_core), range(n_high), range(n_row)):
        group = []
        for low in range(n_low):
            run = (high + (core == 1 and low < n_low // 2)) % n_high
            group.append((((x * n_low + low) * n_core + core) * n_high + run) * n_row + row)
        groups.append(group)
    return groups


def swap_rows(rows, outer, inner, unit):
    out = lax.broadcasted_iota(jnp.int32, (rows, rows), 0)
    local = out % (outer * inner * unit)
    source = out - local + (local // unit % inner * outer + local // (unit * inner)) * unit + local % unit
    return (source == lax.broadcasted_iota(jnp.int32, (rows, rows), 1)).astype(jnp.bfloat16)


def product(left, right, contract=(1, 0)):
    return lax.dot_general(
        left, right, (((contract[0],), (contract[1],)), ((), ())), preferred_element_type=jnp.float32
    )


def column(row):
    n = row.shape[1]
    diagonal = lax.broadcasted_iota(jnp.int32, (n, n), 0) == lax.broadcasted_iota(jnp.int32, (n, n), 1)
    values = jnp.broadcast_to(row.astype(jnp.float32), (n, n))
    return jnp.sum(jnp.where(diagonal, values, 0.0), axis=1, keepdims=True)


def send_kernel(n_row, n_low, n_core, n_x, capacity, *refs):
    sources, (out_ref, score_ref), buffers, sems = refs[:4], refs[4:6], refs[6:10], refs[10]
    copies = [pltpu.make_async_copy(sources[i], buffers[i], sems.at[i]) for i in range(4)]
    for copy in copies:
        copy.start()
    for copy in copies:
        copy.wait()
    tokens_ref, expert_ref, slot_ref, router_ref = buffers
    tok_rows, width = tokens_ref.shape
    piece = width // n_row
    expert = expert_ref[...]
    chip, core = lax.div(expert, n_core), lax.rem(expert, n_core)
    place = (lax.rem(chip, n_low) * n_x + lax.div(chip, n_low)) * n_core + core
    experts = column(expert)
    code = column(place * capacity + slot_ref[...])
    logits = product(tokens_ref[...], router_ref[...], (1, 1))
    numbers = lax.broadcasted_iota(jnp.int32, logits.shape, 1).astype(jnp.float32)
    picked = jnp.sum(jnp.where(numbers == experts, logits, 0.0), axis=1, keepdims=True)
    score = jax.nn.sigmoid(picked)
    score_ref[...] = jnp.broadcast_to(score, score_ref.shape)
    codes = jnp.broadcast_to(code, (tok_rows, CODE_COLUMNS)).astype(jnp.bfloat16)
    for y in range(n_row):
        cut = pl.ds(y * piece, piece)
        scaled = (score * tokens_ref[:, cut].astype(jnp.float32)).astype(jnp.bfloat16)
        for high in range(out_ref.shape[0] // n_row):
            out_ref[high * n_row + y, :, pl.ds(0, piece)] = scaled
            out_ref[high * n_row + y, :, pl.ds(piece, CODE_COLUMNS)] = codes


def spread_kernel(order, rows_ref, out_ref):
    ordered = product(swap_rows(*order), rows_ref[...]).astype(jnp.bfloat16)
    for y in range(out_ref.shape[0]):
        out_ref[y] = ordered


def collect_kernel(order, parts_ref, out_ref):
    swap = swap_rows(*order)
    total = product(swap, parts_ref[0])
    for y in range(1, parts_ref.shape[0]):
        total += product(swap, parts_ref[y])
    out_ref[...] = total.astype(jnp.bfloat16)


def expert_kernel(order, back, rows_ref, hidden_ref, gate_ref, up_ref, act_ref, out_ref):
    n_row, _, piece = rows_ref.shape
    cuts = [pl.ds(y * piece, piece) for y in range(n_row)]
    cotangent = product(swap_rows(*order), hidden_ref[...])
    gate_proj = jnp.zeros(act_ref.shape, jnp.float32)
    lifted = gate_proj
    for y in range(n_row):
        gate_proj += product(rows_ref[y], gate_ref[cuts[y], :])
        lifted += product(rows_ref[y], up_ref[cuts[y], :])
    sigma_gate = jax.nn.sigmoid(gate_proj)
    silu_gate = gate_proj * sigma_gate
    silu_slope = sigma_gate * (1.0 + gate_proj * (1.0 - sigma_gate))
    activation = (silu_gate * lifted).astype(jnp.bfloat16)
    d_gate = (cotangent * lifted * silu_slope).astype(jnp.bfloat16)
    d_lifted = (cotangent * silu_gate).astype(jnp.bfloat16)
    for y in range(n_row):
        part = product(d_gate, gate_ref[cuts[y], :], (1, 1))
        part += product(d_lifted, up_ref[cuts[y], :], (1, 1))
        out_ref[y] = part.astype(jnp.bfloat16)
    act_ref[...] = product(swap_rows(*back), activation).astype(jnp.bfloat16)


VMEM_SPEC = pl.BlockSpec(memory_space=pltpu.VMEM)


def local_call(kernel, shape, inputs, flops, limit):
    moved = 2 * (math.prod(shape) + sum(value.size for value in inputs))
    return pl.pallas_call(
        kernel,
        out_shape=jax.ShapeDtypeStruct(shape, jnp.bfloat16),
        in_specs=[VMEM_SPEC] * len(inputs),
        out_specs=VMEM_SPEC,
        compiler_params=pltpu.CompilerParams(vmem_limit_bytes=limit),
        cost_estimate=pl.CostEstimate(flops=flops, bytes_accessed=moved, transcendentals=0),
    )(*inputs)


def run_expert(order, back, rows, hidden, gate_weight, up_weight):
    n_row, rows_all, piece = rows.shape
    width, units = gate_weight.shape
    return pl.pallas_call(
        functools.partial(expert_kernel, order, back),
        out_shape=(
            jax.ShapeDtypeStruct(hidden.shape, jnp.bfloat16),
            jax.ShapeDtypeStruct(rows.shape, jnp.bfloat16),
        ),
        in_specs=[VMEM_SPEC] * 4,
        out_specs=(VMEM_SPEC, VMEM_SPEC),
        compiler_params=pltpu.CompilerParams(vmem_limit_bytes=24 << 20),
        cost_estimate=pl.CostEstimate(
            flops=8 * rows_all * width * units, bytes_accessed=4 * width * units, transcendentals=rows_all * units
        ),
    )(rows, hidden, gate_weight, up_weight)


def shards(tokens, expert_ids, slot_ids, router, w_gate, w_up, hidden_grad):
    n_x, n_low, n_core, n_high, n_row = (lax.axis_size(axis) for axis in AXES)
    n_tensor = n_high * n_row
    n_expert = n_x * n_low * n_core
    tok_rows, width = tokens.shape
    experts_all = router.shape[1]
    rows_all = hidden_grad.shape[1]
    capacity = rows_all // n_expert
    piece = width // n_row
    group = n_tensor * tok_rows
    gate_weight, up_weight = w_gate[0], w_up[0]

    outgoing, scores = pl.pallas_call(
        functools.partial(send_kernel, n_row, n_low, n_core, n_x, capacity),
        out_shape=(
            jax.ShapeDtypeStruct((n_tensor, tok_rows, piece + CODE_COLUMNS), jnp.bfloat16),
            jax.ShapeDtypeStruct((tok_rows, CODE_COLUMNS), jnp.float32),
        ),
        in_specs=[pl.BlockSpec(memory_space=pltpu.HBM)] * 4,
        out_specs=(VMEM_SPEC, VMEM_SPEC),
        scratch_shapes=[
            pltpu.VMEM((tok_rows, width), jnp.bfloat16),
            pltpu.VMEM((1, tok_rows), jnp.int32),
            pltpu.VMEM((1, tok_rows), jnp.int32),
            pltpu.VMEM((experts_all, width), jnp.bfloat16),
            pltpu.SemaphoreType.DMA((4,)),
        ],
        compiler_params=pltpu.CompilerParams(vmem_limit_bytes=WHOLE_VMEM),
        cost_estimate=pl.CostEstimate(
            flops=2 * tok_rows * width * experts_all, bytes_accessed=2 * width * experts_all, transcendentals=tok_rows
        ),
    )(tokens, expert_ids.reshape(1, tok_rows), slot_ids.reshape(1, tok_rows), router.T)
    router_score = scores[:, 0]
    picked_mask = expert_ids[:, None] == jnp.arange(experts_all, dtype=jnp.int32)[None, :]
    token_float = tokens.astype(jnp.float32)
    group_rows = exchange(outgoing, ("high", "row")).reshape(group, piece + CODE_COLUMNS)

    slot_numbers = jnp.arange(experts_all * capacity, dtype=jnp.int32)
    placed = group_rows[:, piece : piece + 1].astype(jnp.int32) == slot_numbers[None, :]
    placed = placed.astype(jnp.bfloat16)
    slots = lax.dot_general(
        placed, group_rows[:, :piece], (((0,), (0,)), ((), ())), preferred_element_type=jnp.float32
    ).astype(jnp.bfloat16)
    groups = window_groups()
    n_side = n_x * n_core
    block = n_low * capacity
    side_first = (rows_all, n_side, n_low, capacity)
    low_first = (rows_all, n_low, n_side, capacity)
    swap_flops = 2 * rows_all * rows_all * piece
    rows = exchange(slots.reshape(n_low, n_side * capacity, piece), AXES, groups).reshape(rows_all, piece)
    rows = local_call(
        functools.partial(spread_kernel, side_first), (n_row, rows_all, piece), [rows], swap_flops, 8 << 20
    )
    arrived = exchange(rows.reshape(n_row * n_side, block, piece), ("row", "x", "core"))

    activation, partial = run_expert(
        (rows_all, n_core, n_low, capacity),
        (rows_all, n_low, n_core, capacity),
        arrived.reshape(n_row, rows_all, piece),
        hidden_grad[0],
        gate_weight,
        up_weight,
    )

    partial = exchange(partial.reshape(n_row * n_side, block, piece), ("row", "x", "core"))
    summed = local_call(
        functools.partial(collect_kernel, low_first),
        (rows_all, piece),
        [partial.reshape(n_row, rows_all, piece)],
        n_row * swap_flops,
        8 << 20,
    )
    summed = summed.reshape(n_low, n_side * capacity, piece)
    returned = exchange(summed, AXES, groups).reshape(experts_all * capacity, piece)
    mine = jnp.dot(placed, returned, preferred_element_type=jnp.float32).astype(jnp.bfloat16)
    home = exchange(mine.reshape(n_tensor, tok_rows, piece), ("high", "row"))
    home = jnp.sum(home.reshape(n_high, n_row, tok_rows, piece).astype(jnp.float32), axis=0)
    d_float = home.transpose(1, 0, 2).reshape(tok_rows, width).astype(jnp.bfloat16).astype(jnp.float32)

    inner = jnp.sum(token_float * d_float, axis=1)
    router_column = lax.dot_general(
        picked_mask.astype(jnp.bfloat16), router, (((1,), (1,)), ((), ())), preferred_element_type=jnp.float32
    )
    gradient = (
        router_score[:, None] * d_float
        + (inner * router_score * (1.0 - router_score))[:, None] * router_column
    )
    return activation[None], gradient.astype(jnp.bfloat16)


def solution(mesh):
    n_expert, n_tensor = mesh.devices.shape
    n_row = n_x = math.isqrt(n_tensor)
    split = Mesh(mesh.devices.reshape(n_x, n_expert // (2 * n_x), 2, n_tensor // n_row, n_row), AXES)
    expert, tensor = AXES[:3], AXES[3:]
    in_specs = (
        P(AXES, None),
        P(AXES),
        P(AXES),
        P(),
        P(expert, None, tensor),
        P(expert, None, tensor),
        P(expert, None, tensor),
    )
    out_specs = (P(expert, None, tensor), P(AXES, None))
    return jax.shard_map(shards, mesh=split, in_specs=in_specs, out_specs=out_specs, check_vma=False)
```

```python
import functools
import itertools
import math

import jax
import jax.numpy as jnp
from jax import lax
from jax.experimental import pallas as pl
from jax.experimental.pallas import tpu as pltpu
from jax.sharding import Mesh
from jax.sharding import PartitionSpec as P

CODE_COLUMNS = 128
WHOLE_VMEM = 66_500_000


AXES = ("x", "low", "core", "high", "row")


def exchange(buffer, axes, groups=None):
    return lax.all_to_all(buffer, axes, split_axis=0, concat_axis=0, axis_index_groups=groups, tiled=True)


def window_groups():
    n_x, n_low, n_core, n_high, n_row = (lax.axis_size(axis) for axis in AXES)
    groups = []
    for core, high, row in itertools.product(range(n_core), range(n_high), range(n_row)):
        group = []
        for x, low in itertools.product(range(n_x), range(n_low)):
            run = (high + (core == 1 and low < n_low // 2)) % n_high
            group.append((((x * n_low + low) * n_core + core) * n_high + run) * n_row + row)
        groups.append(group)
    return groups


def swap_rows(rows, outer, inner, unit):
    out = lax.broadcasted_iota(jnp.int32, (rows, rows), 0)
    source = (out // unit % inner * outer + out // (unit * inner)) * unit + out % unit
    return (source == lax.broadcasted_iota(jnp.int32, (rows, rows), 1)).astype(jnp.bfloat16)


def product(left, right, contract=(1, 0)):
    return lax.dot_general(
        left, right, (((contract[0],), (contract[1],)), ((), ())), preferred_element_type=jnp.float32
    )


def column(row):
    n = row.shape[1]
    diagonal = lax.broadcasted_iota(jnp.int32, (n, n), 0) == lax.broadcasted_iota(jnp.int32, (n, n), 1)
    values = jnp.broadcast_to(row.astype(jnp.float32), (n, n))
    return jnp.sum(jnp.where(diagonal, values, 0.0), axis=1, keepdims=True)


def send_kernel(n_row, capacity, *refs):
    sources, (out_ref, score_ref), buffers, sems = refs[:4], refs[4:6], refs[6:10], refs[10]
    copies = [pltpu.make_async_copy(sources[i], buffers[i], sems.at[i]) for i in range(4)]
    for copy in copies:
        copy.start()
    for copy in copies:
        copy.wait()
    tokens_ref, expert_ref, slot_ref, router_ref = buffers
    tok_rows, width = tokens_ref.shape
    piece = width // n_row
    experts = column(expert_ref[...])
    code = experts * capacity + column(slot_ref[...])
    logits = product(tokens_ref[...], router_ref[...], (1, 1))
    numbers = lax.broadcasted_iota(jnp.int32, logits.shape, 1).astype(jnp.float32)
    picked = jnp.sum(jnp.where(numbers == experts, logits, 0.0), axis=1, keepdims=True)
    score = jax.nn.sigmoid(picked)
    score_ref[...] = jnp.broadcast_to(score, score_ref.shape)
    codes = jnp.broadcast_to(code, (tok_rows, CODE_COLUMNS)).astype(jnp.bfloat16)
    for y in range(n_row):
        cut = pl.ds(y * piece, piece)
        scaled = (score * tokens_ref[:, cut].astype(jnp.float32)).astype(jnp.bfloat16)
        for high in range(out_ref.shape[0] // n_row):
            peer = y * (out_ref.shape[0] // n_row) + high
            out_ref[peer, :, pl.ds(0, piece)] = scaled
            out_ref[peer, :, pl.ds(piece, CODE_COLUMNS)] = codes


def spread_kernel(order, rows_ref, out_ref):
    ordered = product(swap_rows(*order), rows_ref[...]).astype(jnp.bfloat16)
    peers, half, _ = out_ref.shape
    n_row = peers * half // ordered.shape[0]
    for peer in range(peers):
        out_ref[peer] = ordered[peer // n_row * half : (peer // n_row + 1) * half]


def all_cores(ref, n_row, y):
    return jnp.concatenate([ref[peer] for peer in range(y, ref.shape[0], n_row)], axis=0)


def collect_kernel(order, parts_ref, out_ref):
    swap = swap_rows(*order)
    n_row = parts_ref.shape[0] * parts_ref.shape[1] // out_ref.shape[0]
    total = product(swap, all_cores(parts_ref, n_row, 0))
    for y in range(1, n_row):
        total += product(swap, all_cores(parts_ref, n_row, y))
    out_ref[...] = total.astype(jnp.bfloat16)


def expert_kernel(order, back, rows_ref, hidden_ref, gate_ref, up_ref, act_ref, out_ref):
    peers, half, piece = rows_ref.shape
    n_row = peers * half // hidden_ref.shape[0]
    cuts = [pl.ds(y * piece, piece) for y in range(n_row)]
    cotangent = product(swap_rows(*order), hidden_ref[...])
    gate_proj = jnp.zeros(act_ref.shape, jnp.float32)
    lifted = gate_proj
    for y in range(n_row):
        rows = all_cores(rows_ref, n_row, y)
        gate_proj += product(rows, gate_ref[cuts[y], :])
        lifted += product(rows, up_ref[cuts[y], :])
    sigma_gate = jax.nn.sigmoid(gate_proj)
    silu_gate = gate_proj * sigma_gate
    silu_slope = sigma_gate * (1.0 + gate_proj * (1.0 - sigma_gate))
    activation = (silu_gate * lifted).astype(jnp.bfloat16)
    d_gate = (cotangent * lifted * silu_slope).astype(jnp.bfloat16)
    d_lifted = (cotangent * silu_gate).astype(jnp.bfloat16)
    for y in range(n_row):
        part = product(d_gate, gate_ref[cuts[y], :], (1, 1))
        part += product(d_lifted, up_ref[cuts[y], :], (1, 1))
        part = part.astype(jnp.bfloat16)
        for core in range(peers // n_row):
            out_ref[core * n_row + y] = part[core * half : (core + 1) * half]
    act_ref[...] = product(swap_rows(*back), activation).astype(jnp.bfloat16)


VMEM_SPEC = pl.BlockSpec(memory_space=pltpu.VMEM)


def local_call(kernel, shape, inputs, flops, limit):
    moved = 2 * (math.prod(shape) + sum(value.size for value in inputs))
    return pl.pallas_call(
        kernel,
        out_shape=jax.ShapeDtypeStruct(shape, jnp.bfloat16),
        in_specs=[VMEM_SPEC] * len(inputs),
        out_specs=VMEM_SPEC,
        compiler_params=pltpu.CompilerParams(vmem_limit_bytes=limit),
        cost_estimate=pl.CostEstimate(flops=flops, bytes_accessed=moved, transcendentals=0),
    )(*inputs)


def run_expert(order, back, rows, hidden, gate_weight, up_weight):
    rows_all = hidden.shape[0]
    width, units = gate_weight.shape
    return pl.pallas_call(
        functools.partial(expert_kernel, order, back),
        out_shape=(
            jax.ShapeDtypeStruct(hidden.shape, jnp.bfloat16),
            jax.ShapeDtypeStruct(rows.shape, jnp.bfloat16),
        ),
        in_specs=[VMEM_SPEC] * 4,
        out_specs=(VMEM_SPEC, VMEM_SPEC),
        compiler_params=pltpu.CompilerParams(vmem_limit_bytes=24 << 20),
        cost_estimate=pl.CostEstimate(
            flops=8 * rows_all * width * units, bytes_accessed=4 * width * units, transcendentals=rows_all * units
        ),
    )(rows, hidden, gate_weight, up_weight)


def shards(tokens, expert_ids, slot_ids, router, w_gate, w_up, hidden_grad):
    n_x, n_low, n_core, n_high, n_row = (lax.axis_size(axis) for axis in AXES)
    n_chip, n_tensor = n_x * n_low, n_high * n_row
    n_expert = n_chip * n_core
    tok_rows, width = tokens.shape
    experts_all = router.shape[1]
    rows_all = hidden_grad.shape[1]
    capacity = rows_all // n_expert
    piece = width // n_row
    group = n_tensor * tok_rows
    gate_weight, up_weight = w_gate[0], w_up[0]

    outgoing, scores = pl.pallas_call(
        functools.partial(send_kernel, n_row, capacity),
        out_shape=(
            jax.ShapeDtypeStruct((n_tensor, tok_rows, piece + CODE_COLUMNS), jnp.bfloat16),
            jax.ShapeDtypeStruct((tok_rows, CODE_COLUMNS), jnp.float32),
        ),
        in_specs=[pl.BlockSpec(memory_space=pltpu.HBM)] * 4,
        out_specs=(VMEM_SPEC, VMEM_SPEC),
        scratch_shapes=[
            pltpu.VMEM((tok_rows, width), jnp.bfloat16),
            pltpu.VMEM((1, tok_rows), jnp.int32),
            pltpu.VMEM((1, tok_rows), jnp.int32),
            pltpu.VMEM((experts_all, width), jnp.bfloat16),
            pltpu.SemaphoreType.DMA((4,)),
        ],
        compiler_params=pltpu.CompilerParams(vmem_limit_bytes=WHOLE_VMEM),
        cost_estimate=pl.CostEstimate(
            flops=2 * tok_rows * width * experts_all, bytes_accessed=2 * width * experts_all, transcendentals=tok_rows
        ),
    )(tokens, expert_ids.reshape(1, tok_rows), slot_ids.reshape(1, tok_rows), router.T)
    router_score = scores[:, 0]
    picked_mask = expert_ids[:, None] == jnp.arange(experts_all, dtype=jnp.int32)[None, :]
    token_float = tokens.astype(jnp.float32)
    group_rows = exchange(outgoing, ("row", "high")).reshape(group, piece + CODE_COLUMNS)

    slot_numbers = jnp.arange(experts_all * capacity, dtype=jnp.int32)
    placed = group_rows[:, piece : piece + 1].astype(jnp.int32) == slot_numbers[None, :]
    placed = placed.astype(jnp.bfloat16)
    slots = lax.dot_general(
        placed, group_rows[:, :piece], (((0,), (0,)), ((), ())), preferred_element_type=jnp.float32
    ).astype(jnp.bfloat16)
    groups = window_groups()
    core_first = (rows_all, n_core, n_chip, capacity)
    chip_first = (rows_all, n_chip, n_core, capacity)
    half = rows_all // n_core
    swap_flops = 2 * rows_all * rows_all * piece
    chips = exchange(slots.reshape(n_chip, n_core * capacity, piece), AXES, groups).reshape(rows_all, piece)
    chips = local_call(
        functools.partial(spread_kernel, core_first), (n_core * n_row, half, piece), [chips], swap_flops, 8 << 20
    )
    arrived = exchange(chips, ("core", "row"))

    activation, partial = run_expert(
        core_first, chip_first, arrived, hidden_grad[0], gate_weight, up_weight
    )

    partial = exchange(partial, ("core", "row"))
    summed = local_call(
        functools.partial(collect_kernel, chip_first),
        (rows_all, piece),
        [partial],
        n_row * swap_flops,
        8 << 20,
    )
    summed = summed.reshape(n_chip, n_core * capacity, piece)
    returned = exchange(summed, AXES, groups).reshape(experts_all * capacity, piece)
    mine = jnp.dot(placed, returned, preferred_element_type=jnp.float32).astype(jnp.bfloat16)
    home = exchange(mine.reshape(n_tensor, tok_rows, piece), ("row", "high"))
    home = jnp.sum(home.reshape(n_row, n_high, tok_rows, piece).astype(jnp.float32), axis=1)
    d_float = home.transpose(1, 0, 2).reshape(tok_rows, width).astype(jnp.bfloat16).astype(jnp.float32)

    inner = jnp.sum(token_float * d_float, axis=1)
    router_column = lax.dot_general(
        picked_mask.astype(jnp.bfloat16), router, (((1,), (1,)), ((), ())), preferred_element_type=jnp.float32
    )
    gradient = (
        router_score[:, None] * d_float
        + (inner * router_score * (1.0 - router_score))[:, None] * router_column
    )
    return activation[None], gradient.astype(jnp.bfloat16)


def solution(mesh):
    n_expert, n_tensor = mesh.devices.shape
    n_row = n_x = math.isqrt(n_tensor)
    split = Mesh(mesh.devices.reshape(n_x, n_expert // (2 * n_x), 2, n_tensor // n_row, n_row), AXES)
    expert, tensor = AXES[:3], AXES[3:]
    in_specs = (
        P(AXES, None),
        P(AXES),
        P(AXES),
        P(),
        P(expert, None, tensor),
        P(expert, None, tensor),
        P(expert, None, tensor),
    )
    out_specs = (P(expert, None, tensor), P(AXES, None))
    return jax.shard_map(shards, mesh=split, in_specs=in_specs, out_specs=out_specs, check_vma=False)
```
